32 devices in a mesh: rep: 2 (over x), seq: 16 (over z, y, core).
Axes of the slice: x: 2, y: 2, z: 4, core: 2. Of those that a mesh axis runs over, the one named last changes fastest.
Arguments:
- cached_keys: bfloat16 [32768, 1024], P(('rep', 'seq')), parts along dimension 0, may hold values from -6 to 6
- cached_values: bfloat16 [32768, 1024], P(('rep', 'seq')), parts along dimension 0, may hold values from -6 to 6
- window_queries: bfloat16 [256, 8192], P(('rep', 'seq')), parts along dimension 0
- kept_count: int32 [32], P(('rep', 'seq')), parts along dimension 0, may hold values from 1 to 640, 8192 in all
- kept_entry: int32 [20480], P(('rep', 'seq')), parts along dimension 0, may hold values from 0 to 8191
- row_owner: int32 [20480], P(('rep', 'seq')), parts along dimension 0, may hold values from 0 to 15, as said below
Outputs:
- importance: float32 [16, 16384], P('rep', 'seq'), parts along dimension 0
- compact_rows: bfloat16 [20480, 256], P(('rep', 'seq')), parts along dimension 0
- compact_score: bfloat16 [20480], P(('rep', 'seq')), parts along dimension 0
The draws below stay inside these ranges and needn't reach their ends.
There are 2 independent parts, one for each index of `rep`. The reference program is written for one: setup_inputs(seed, part) draws one part's arguments, and reference() takes and returns one part's arrays. A program takes and returns all parts, laid end to end along the dimension named above; each array names one. Nothing has to cross between parts.
Inputs may be any that keep to these rules, and one draw needn't show every extreme that they name: `kept_count`: the counts of the 16 devices sum to 8192. `kept_entry`: entries may repeat. `row_owner`: among the 640 slots of one device every owner is named by exactly 40 slots.
All inputs are finite; a program needn't handle non-finite values.
Results may differ from the reference program's by a relative error of at most 0.0004.
Values may be sent and summed in bfloat16 or wider, within the bound.
A program may use at most 64 MiB of HBM per device.

```python
import math
import jax
import jax.numpy as jnp
import numpy as np
from jax import lax

HEADS = 64
KV_HEADS = 8
HEAD_DIM = 128
GROUP = 8
WINDOW = 128
POOL = 7
TOK_DEV = 1024
SEQ = 16384
SLOTS = 640
CAP = 40
KEPT = 8192
N_SEQ = 16


def draw_cached_keys(key, part):
    return jnp.clip(jax.random.normal(jax.random.fold_in(key, 3), (SEQ, KV_HEADS * HEAD_DIM), jnp.float32), -6.0, 6.0).astype(jnp.bfloat16)


def draw_window_queries(key, part):
    return jnp.clip(jax.random.normal(jax.random.fold_in(key, 5), (WINDOW, HEADS * HEAD_DIM), jnp.float32), -6.0, 6.0).astype(jnp.bfloat16)


def draw_row_owner(key, part):
    peers = N_SEQ
    filled = jnp.tile(jnp.arange(peers, dtype=jnp.int32)[None, :], (peers, CAP))
    shuffle = jax.random.randint(jax.random.fold_in(key, 23), (peers, SLOTS), 0, 2 ** 19) * SLOTS + jnp.arange(SLOTS)[None, :]
    order = jnp.argsort(shuffle, axis=1, stable=True)
    return jnp.take_along_axis(filled, order, axis=1).reshape(-1).astype(jnp.int32)


def set_ends(values, own_key, smallest, top_value):
    longest = values.shape.index(max(values.shape))
    spots = []
    for shift in (0, 1):
        where = [jax.random.randint(jax.random.fold_in(own_key, axis), (), 0, length) for axis, length in enumerate(values.shape)]
        where[longest] = (where[longest] + shift) % values.shape[longest]
        spots.append(tuple(where))
    return values.at[spots[0]].set(smallest).at[spots[1]].set(top_value)


def levels(key, shape, pieces, low, largest):
    gain, own = 1.0, jax.random.fold_in(key, 6)
    for position, blocks in pieces:
        steps = jnp.exp(jax.random.uniform(jax.random.fold_in(own, position), (blocks,), jnp.float32, low / len(pieces), largest / len(pieces)))
        gain = gain * jnp.repeat(steps, shape[position] // blocks).reshape([-1 if axis == position else 1 for axis in range(len(shape))])
    return gain


def split_up(amount, total, bound, slope):
    portions = [(1 << 20) // math.isqrt(standing ** slope) + 1 for standing in range(2, amount + 1)]
    spare, given = total - bound - (amount - 1), [1] * (amount - 1)
    while spare > 0:
        candidates = [i for i in range(amount - 1) if given[i] < bound]
        pool, remaining = sum([portions[i] for i in candidates]), spare
        for i in candidates:
            addition = min(bound - given[i], max(1, remaining * portions[i] // pool), spare)
            given[i] = given[i] + addition
            spare = spare - addition
    return np.array([bound] + given)


def ragged_sizes(rng, number_of, total, most, slope):
    if number_of == 2:
        one = jax.random.randint(rng, (), max(1, total - most), min(most, total - 1) + 1)
        return jnp.stack([one, total - one])
    sizes = jnp.asarray(split_up(number_of, total, most, slope), jnp.int32)
    twos = (number_of - 1) // 2
    giver, sink = sizes[1:1 + 2 * twos:2], sizes[2:2 + 2 * twos:2]
    room = jnp.minimum(giver - 1, most - sink)
    moved = jax.random.randint(jax.random.fold_in(rng, 1), (twos,), 0, 1 << 20) % (room + 1)
    sizes = sizes.at[1:1 + 2 * twos:2].set(giver - moved).at[2:2 + 2 * twos:2].set(sink + moved)
    return sizes[jax.random.permutation(jax.random.fold_in(rng, 2), number_of)]


def bell_draw(rng, dims, spread, most, shards=(), kind=jnp.bfloat16):
    loudness = levels(rng, dims, shards, -0.22, 0.18) if shards else 1.0
    result = jax.random.normal(rng, dims, jnp.float32) * spread * loudness
    return jnp.minimum(jnp.maximum(result, -most), most).astype(kind)


def setup_inputs(seed: int = 0, part: int = 0) -> dict:
    splits = jax.random.split(jax.random.key(seed), 7)
    part_splits = jax.random.split(jax.random.fold_in(splits[6], part), 7)
    return {
        "cached_keys": draw_cached_keys(jax.random.fold_in(jax.random.fold_in(splits[6], part), 71), part),
        "cached_values": bell_draw(part_splits[1], (SEQ, KV_HEADS * HEAD_DIM), 1.0, 6.0, ((0, 16),)),
        "window_queries": draw_window_queries(jax.random.fold_in(jax.random.fold_in(splits[6], part), 71), part),
        "kept_count": ragged_sizes(part_splits[3], N_SEQ, KEPT, SLOTS, 2).astype(jnp.int32),
        "kept_entry": set_ends(jax.random.randint(part_splits[4], (N_SEQ * SLOTS,), 0, KV_HEADS * TOK_DEV), jax.random.fold_in(part_splits[4], 1), 0, (KV_HEADS * TOK_DEV) - 1).astype(jnp.int32),
        "row_owner": draw_row_owner(jax.random.fold_in(jax.random.fold_in(splits[6], part), 71), part),
    }


def window_groups(window_queries):
    shaped = window_queries.reshape(WINDOW, KV_HEADS, GROUP, HEAD_DIM).transpose(1, 2, 0, 3)
    return shaped.reshape(KV_HEADS, GROUP * WINDOW, HEAD_DIM).astype(jnp.float32)


def block_scores(query_groups, key_block):
    return jnp.einsum("gqd,gtd->gqt", query_groups, key_block.astype(jnp.float32)) * (HEAD_DIM ** -0.5)


def reference(cached_keys, cached_values, window_queries, kept_count, kept_entry, row_owner):
    query_groups = window_groups(window_queries)
    key_blocks = cached_keys.reshape(N_SEQ, TOK_DEV, KV_HEADS, HEAD_DIM).transpose(0, 2, 1, 3)

    def stat_step(carry, key_block):
        run_peak, run_total = carry
        scores = block_scores(query_groups, key_block)
        new_peak = jnp.maximum(run_peak, jnp.max(scores, axis=2))
        run_total = run_total * jnp.exp(run_peak - new_peak) + jnp.sum(jnp.exp(scores - new_peak[:, :, None]), axis=2)
        return (new_peak, run_total), None

    initial = (jnp.full((KV_HEADS, GROUP * WINDOW), -jnp.inf, jnp.float32), jnp.zeros((KV_HEADS, GROUP * WINDOW), jnp.float32))
    (glob_peak, glob_total), _ = lax.scan(stat_step, initial, key_blocks)
    inverse = 1.0 / glob_total

    def mass_step(carry, key_block):
        scores = block_scores(query_groups, key_block)
        return carry, jnp.sum(jnp.exp(scores - glob_peak[:, :, None]) * inverse[:, :, None], axis=1)

    _, column_mass = lax.scan(mass_step, jnp.zeros((), jnp.float32), key_blocks)
    column_mass = column_mass.transpose(1, 0, 2).reshape(KV_HEADS, SEQ)
    margin = POOL // 2
    padded = jnp.pad(column_mass, ((0, 0), (margin, margin)))
    pooled = padded[:, 0:SEQ]
    for offset in range(1, POOL):
        pooled = pooled + padded[:, offset:offset + SEQ]
    importance = pooled * (SEQ / (GROUP * WINDOW * POOL))

    everything = jnp.arange(N_SEQ * SLOTS, dtype=jnp.int32)
    device = everything // SLOTS
    within = everything % SLOTS
    is_live = within < kept_count[device]
    member = ((row_owner[:, None] == jnp.arange(N_SEQ, dtype=jnp.int32)[None, :]) & is_live[:, None]).astype(jnp.int32)
    member = member.reshape(N_SEQ, SLOTS, N_SEQ)
    earlier = jnp.cumsum(member, axis=1) - member
    slot_rank = jnp.sum(earlier * member, axis=2).reshape(-1)
    head_index = kept_entry // TOK_DEV
    token_index = device * TOK_DEV + kept_entry % TOK_DEV
    row_index = token_index * KV_HEADS + head_index
    key_rows = cached_keys.reshape(SEQ * KV_HEADS, HEAD_DIM)[row_index]
    value_rows = cached_values.reshape(SEQ * KV_HEADS, HEAD_DIM)[row_index]
    payload = jnp.concatenate([key_rows, value_rows], axis=1)
    score_rows = importance[head_index, token_index].astype(jnp.bfloat16)
    total_rows = N_SEQ * N_SEQ * CAP
    target = jnp.where(is_live, row_owner * (N_SEQ * CAP) + device * CAP + slot_rank, total_rows)
    compact_rows = jnp.zeros((total_rows, 2 * HEAD_DIM), jnp.bfloat16).at[target].set(payload, mode="drop")
    compact_score = jnp.zeros((total_rows,), jnp.bfloat16).at[target].set(score_rows, mode="drop")
    return importance, compact_rows, compact_score
```

```python
import functools

import jax
import jax.numpy as jnp
from jax import lax
from jax.experimental import pallas as pl
from jax.experimental.pallas import tpu as pltpu
from jax.sharding import PartitionSpec as P

KV_HEADS = 8
GROUP = 8
HEAD_DIM = 128
POOL = 7
LANES = 128
MESH = pl.DeviceIdType.MESH
NT = (((1,), (1,)), ((), ()))


def iota(shape, dim):
    return lax.broadcasted_iota(jnp.int32, shape, dim)


def kernel(
    n, cap, cap_pad, pool_scale,
    keys_hbm, vals_hbm, wq_hbm, count_ref, entry_ref, owner_ref,
    imp_ref, rows_out, score_out,
    keys, vals, qall, ebuf, stat, stat_in, glob, rows_send, onehot, head_hot, mass, halo, ssend, srecv,
    zs, zr, ys, yr, bs, br, ts, tr, gs, gr, rs, rr, hs, hr, ss, sr, ls,
):
    G = KV_HEADS
    me = lax.axis_index("seq")
    A = n // 4
    a, b, c = me // 4, (me // 2) % 2, me % 2
    slots = entry_ref.shape[1]
    positions = keys.shape[0]
    out_slots = n * cap_pad
    qrows = qall.shape[4]
    scale = HEAD_DIM ** (-0.5)
    per_owner = n // G

    def stat_owner(g):
        return (g * per_owner + n // 2) % n

    def to(index):
        return {"seq": index}

    def remote(src, dst, ssem, rsem, index):
        return pltpu.make_async_remote_copy(
            src_ref=src, dst_ref=dst, send_sem=ssem, recv_sem=rsem,
            device_id=to(index), device_id_type=MESH,
        )

    def drain(region, sem):
        pltpu.make_async_copy(region, region, sem).wait()

    key_copy = pltpu.make_async_copy(keys_hbm, keys, ls.at[0])
    val_copy = pltpu.make_async_copy(vals_hbm, vals, ls.at[1])
    own_q = pltpu.make_async_copy(wq_hbm, qall.at[:, c, b, a], ls.at[2])
    own_q.start()
    key_copy.start()
    val_copy.start()
    barrier = pltpu.get_barrier_semaphore()

    @pl.loop(1, n)
    def _(k):
        pl.semaphore_signal(barrier, inc=1, device_id=to(lax.rem(me + k, n)), device_id_type=MESH)

    entry = entry_ref[...]
    owner = owner_ref[...]
    live = iota((1, slots), 1) < count_ref[0]
    owner_live = jnp.where(live, owner, -1)
    member = jnp.where(iota((n, slots), 0) == owner_live, 1.0, 0.0)
    before = jnp.where(iota((slots, slots), 0) < iota((slots, slots), 1), 1.0, 0.0).astype(jnp.bfloat16)
    earlier = jnp.dot(member.astype(jnp.bfloat16), before, preferred_element_type=jnp.float32)
    rank = jnp.sum(member * earlier, axis=0, keepdims=True)
    target = jnp.where(live, owner * cap_pad + rank.astype(jnp.int32), -1)
    head = jnp.zeros((1, slots), jnp.int32)
    for h in range(1, G):
        head = head + jnp.where(entry >= h * positions, 1, 0)
    token = entry - head * positions
    token_f = (token + 1).astype(jnp.float32)
    head_f = head.astype(jnp.float32)
    head_sel = jnp.where(iota((G, slots), 0) == head, 1.0, 0.0).astype(jnp.bfloat16)
    blk = 256
    for i in range(out_slots // blk):
        hit = (iota((blk, slots), 0) + i * blk) == target
        tok = jnp.sum(jnp.where(hit, token_f, 0.0), axis=1, keepdims=True).astype(jnp.int32) - 1
        onehot[i * blk:(i + 1) * blk, :] = jnp.where(
            iota((blk, positions), 1) == tok, 1.0, 0.0
        ).astype(jnp.bfloat16)
        hit_b = jnp.where(hit, 1.0, 0.0).astype(jnp.bfloat16)
        head_hot[:, i * blk:(i + 1) * blk] = lax.dot_general(
            head_sel, hit_b, NT, preferred_element_type=jnp.float32
        )

    own_q.wait()
    pl.semaphore_wait(barrier, n - 1)

    @pl.loop(0, G)
    def _(g):
        @pl.loop(1, A)
        def _(k):
            peer = lax.rem(a + k, A) * 4 + b * 2 + c
            remote(qall.at[g, c, b, a], qall.at[g, c, b, a], zs.at[g], zr.at[g], peer).start()

    key_copy.wait()
    val_copy.wait()

    for i in range(out_slots // blk):
        hit = (iota((blk, slots), 0) + i * blk) == target
        hcol = jnp.sum(jnp.where(hit, head_f, 0.0), axis=1, keepdims=True).astype(jnp.int32)
        hcol = jnp.broadcast_to(hcol, (blk, HEAD_DIM))
        pick = onehot[i * blk:(i + 1) * blk, :]
        for side, source in enumerate((keys, vals)):
            got = jnp.dot(pick, source[...], preferred_element_type=jnp.float32)
            chosen = jnp.zeros((blk, HEAD_DIM), jnp.float32)
            for h in range(G):
                chosen = jnp.where(hcol == h, got[:, h * HEAD_DIM:(h + 1) * HEAD_DIM], chosen)
            rows_send[
                i * blk:(i + 1) * blk,
                side * HEAD_DIM:(side + 1) * HEAD_DIM,
            ] = chosen.astype(jnp.bfloat16)

    def combine(g):
        @pl.when(me == stat_owner(g))
        def _():
            drain(stat_in.at[pl.ds(0, n - 1)], tr.at[0])
            stat_in[me] = stat[g]
            top = stat_in[0, 0]
            for d in range(1, n):
                top = jnp.maximum(top, stat_in[d, 0])
            total = jnp.zeros_like(top)
            for d in range(n):
                total = total + stat_in[d, 1] * jnp.exp(stat_in[d, 0] - top)
            glob[g, 0] = top
            glob[g, 1] = 1.0 / total

            @pl.loop(1, n)
            def _(k):
                remote(glob.at[g], glob.at[g], gs.at[0], gr.at[g], lax.rem(me + k, n)).start()

    chunk = 2 * LANES
    tblk = 256

    def compute(g):
        group_q = qall.at[g].reshape(qall.shape[1] * qall.shape[2] * A * qrows, HEAD_DIM)
        total_rows = group_q.shape[0]
        key_cols = pl.ds(pl.multiple_of(g * HEAD_DIM, HEAD_DIM), HEAD_DIM)

        @pl.loop(0, total_rows // chunk)
        def _(j):
            qs = group_q[pl.ds(pl.multiple_of(j * chunk, chunk), chunk), :]
            lanes = pl.ds(pl.multiple_of(j * chunk, chunk), chunk)
            top8 = None
            for t in range(positions // tblk):
                s = lax.dot_general(
                    keys[t * tblk:(t + 1) * tblk, key_cols], qs, NT, preferred_element_type=jnp.float32
                )
                ebuf[g, t * tblk:(t + 1) * tblk, lanes] = s
                part = jnp.max(s.reshape(tblk // 8, 8, chunk), axis=0)
                top8 = part if top8 is None else jnp.maximum(top8, part)
            top = jnp.max(top8, axis=0, keepdims=True)
            sum8 = jnp.zeros((8, chunk), jnp.float32)
            for t in range(positions // tblk):
                s = ebuf[g, t * tblk:(t + 1) * tblk, lanes]
                e = jnp.exp((s - top) * scale)
                ebuf[g, t * tblk:(t + 1) * tblk, lanes] = e
                sum8 = sum8 + jnp.sum(e.reshape(tblk // 8, 8, chunk), axis=0)
            total = jnp.sum(sum8, axis=0, keepdims=True)
            top = top * scale
            for i in range(chunk // LANES):
                stat[g, 0, pl.ds(j * (chunk // LANES) + i, 1), :] = top[:, i * LANES:(i + 1) * LANES]
                stat[g, 1, pl.ds(j * (chunk // LANES) + i, 1), :] = total[:, i * LANES:(i + 1) * LANES]

        dest = stat_owner(g)

        @pl.when(me != dest)
        def _():
            remote(stat.at[g], stat_in.at[me], ts.at[g], tr.at[0], dest).start()

    mid_peer = a * 4 + (1 - b) * 2 + c
    core_peer = a * 4 + b * 2 + (1 - c)
    lag = 3

    @pl.loop(0, G + lag)
    def _(step):
        @pl.when(step < G)
        def _():
            g = step
            drain(qall.at[g, c, b, pl.ds(0, A - 1)], zr.at[g])
            remote(qall.at[g, c, b], qall.at[g, c, b], ys.at[g], yr.at[g], mid_peer).start()

        @pl.when((step >= 1) & (step < G + 1))
        def _():
            g = step - 1
            drain(qall.at[g, c, 1 - b], yr.at[g])
            remote(qall.at[g, c], qall.at[g, c], bs.at[g], br.at[g], core_peer).start()

        @pl.when((step >= 2) & (step < G + 2))
        def _():
            g = step - 2
            drain(qall.at[g, 1 - c], br.at[g])
            compute(g)

        @pl.when(step >= 3)
        def _():
            combine(step - 3)

    rows3 = rows_send.reshape(n, cap_pad, 2 * HEAD_DIM)

    @pl.loop(1, n)
    def _(k):
        peer = lax.rem(me + k, n)
        remote(rows3.at[peer], rows_out.at[me], rs.at[0], rr.at[0], peer).start()

    own_rows = pltpu.make_async_copy(rows3.at[me], rows_out.at[me], ls.at[3])
    own_rows.start()

    ones = jnp.ones((8, LANES), jnp.float32)

    @pl.loop(0, G)
    def _(g):
        @pl.when(me != stat_owner(g))
        def _():
            drain(glob.at[g], gr.at[g])

        weight = jnp.exp(stat[g, 0] - glob[g, 0]) * glob[g, 1]
        for t in range(positions // LANES):
            acc = ebuf[g, t * LANES:(t + 1) * LANES, 0:LANES] * weight[0:1, :]
            for k in range(1, weight.shape[0]):
                acc = acc + ebuf[g, t * LANES:(t + 1) * LANES, k * LANES:(k + 1) * LANES] * weight[k:k + 1, :]
            line = lax.dot_general(
                ones, acc, NT, preferred_element_type=jnp.float32, precision=lax.Precision.HIGHEST
            )
            mass[g, :, t * LANES:(t + 1) * LANES] = line[0:1, :]

    halo[0] = jnp.zeros((G, LANES), jnp.float32)
    halo[1] = jnp.zeros((G, LANES), jnp.float32)
    column = jnp.concatenate([mass[g] for g in range(G)], axis=0)
    halo[4] = column[:, 0:LANES]
    halo[5] = column[:, positions - LANES:]
    low_copy = remote(halo.at[4], halo.at[3], hs.at[0], hr.at[0], lax.rem(me + n - 1, n))
    high_copy = remote(halo.at[5], halo.at[2], hs.at[1], hr.at[1], lax.rem(me + 1, n))

    @pl.when(me > 0)
    def _():
        low_copy.start()

    @pl.when(me < n - 1)
    def _():
        high_copy.start()

    @pl.when(me > 0)
    def _():
        drain(halo.at[2], hr.at[1])
        halo[0] = halo[2]

    @pl.when(me < n - 1)
    def _():
        drain(halo.at[3], hr.at[0])
        halo[1] = halo[3]

    padded = jnp.concatenate([halo[0], column, halo[1]], axis=1)
    width = padded.shape[1]
    pooled = padded
    for o in range(1, POOL // 2 + 1):
        pooled = pooled + pltpu.roll(padded, o, 1) + pltpu.roll(padded, width - o, 1)
    importance = pooled[:, LANES:LANES + positions] * pool_scale
    imp_ref[...] = importance

    got = lax.dot_general(
        importance.astype(jnp.bfloat16), onehot[...], NT, preferred_element_type=jnp.float32
    )
    line = jnp.sum(got * head_hot[...], axis=0, keepdims=True)
    owner_of = iota((n, out_slots), 1) - iota((n, out_slots), 0) * cap_pad
    spread = jnp.where((owner_of >= 0) & (owner_of < cap_pad), line, 0.0).astype(jnp.bfloat16)
    row_id, lane_id = iota((out_slots, LANES), 0), iota((out_slots, LANES), 1)
    fold = (row_id - lane_id) % cap_pad == 0
    fold = jnp.where(fold & (lane_id < cap_pad), 1.0, 0.0).astype(jnp.bfloat16)
    table = jnp.dot(spread, fold, preferred_element_type=jnp.float32)
    for k in range(n):
        ssend[k] = table[k:k + 1, :]

    @pl.loop(1, n)
    def _(k):
        peer = lax.rem(me + k, n)
        remote(ssend.at[peer], srecv.at[me], ss.at[0], sr.at[0], peer).start()

    own_rows.wait()
    drain(rows_out.at[pl.ds(0, n - 1)], rr.at[0])
    drain(rows3.at[pl.ds(0, n - 1)], rs.at[0])

    @pl.loop(0, G)
    def _(g):
        drain(qall.at[g, c, b, pl.ds(0, A - 1)], zs.at[g])
        drain(qall.at[g, c, b], ys.at[g])
        drain(qall.at[g, c], bs.at[g])

        @pl.when(me != stat_owner(g))
        def _():
            drain(stat.at[g], ts.at[g])

        @pl.when(me == stat_owner(g))
        def _():
            drain(stat_in.at[pl.ds(0, n - 1)], gs.at[0])

    @pl.when(me > 0)
    def _():
        drain(halo.at[4], hs.at[0])

    @pl.when(me < n - 1)
    def _():
        drain(halo.at[5], hs.at[1])

    drain(ssend.at[pl.ds(0, n - 1)], ss.at[0])
    drain(srecv.at[pl.ds(0, n - 1)], sr.at[0])
    srecv[me] = ssend[me]
    score_out[...] = srecv[...]


def per_device(n, cached_keys, cached_values, window_queries, kept_count, kept_entry, row_owner):
    positions, width = cached_keys.shape
    slots = kept_entry.shape[0]
    cap = slots // n
    cap_pad = -(-cap // 16) * 16
    query_rows = window_queries.shape[0]
    heads = window_queries.shape[1] // HEAD_DIM
    group = heads // KV_HEADS
    window = query_rows * n
    qrows = query_rows * group
    lane_rows = n * qrows // LANES
    wq = (
        window_queries.reshape(query_rows, heads, HEAD_DIM)
        .transpose(1, 0, 2)
        .reshape(KV_HEADS, qrows, HEAD_DIM)
    )
    pool_scale = n * positions / (group * window * POOL)
    any_spec = pl.BlockSpec(memory_space=pl.ANY)
    vmem = pl.BlockSpec(memory_space=pltpu.VMEM)
    dma = pltpu.SemaphoreType.DMA
    A = n // 4
    f32, bf16 = jnp.float32, jnp.bfloat16
    importance, rows, score = pl.pallas_call(
        functools.partial(kernel, n, cap, cap_pad, pool_scale),
        out_shape=(
            jax.ShapeDtypeStruct((KV_HEADS, positions), f32),
            jax.ShapeDtypeStruct((n, cap_pad, 2 * HEAD_DIM), bf16),
            jax.ShapeDtypeStruct((n, 1, LANES), f32),
        ),
        in_specs=[any_spec, any_spec, any_spec, pl.BlockSpec(memory_space=pltpu.SMEM), vmem, vmem],
        out_specs=(vmem, any_spec, vmem),
        scratch_shapes=[
            pltpu.VMEM((positions, width), bf16),
            pltpu.VMEM((positions, width), bf16),
            pltpu.VMEM((KV_HEADS, 2, 2, A, qrows, HEAD_DIM), bf16),
            pltpu.VMEM((KV_HEADS, positions, n * qrows), f32),
            pltpu.VMEM((KV_HEADS, 2, lane_rows, LANES), f32),
            pltpu.VMEM((n, 2, lane_rows, LANES), f32),
            pltpu.VMEM((KV_HEADS, 2, lane_rows, LANES), f32),
            pltpu.VMEM((n * cap_pad, 2 * HEAD_DIM), bf16),
            pltpu.VMEM((n * cap_pad, positions), bf16),
            pltpu.VMEM((KV_HEADS, n * cap_pad), f32),
            pltpu.VMEM((KV_HEADS, 1, positions), f32),
            pltpu.VMEM((6, KV_HEADS, LANES), f32),
            pltpu.VMEM((n, 1, LANES), f32),
            pltpu.VMEM((n, 1, LANES), f32),
        ]
        + [dma((KV_HEADS,))] * 6
        + [dma((KV_HEADS,)), dma((1,)), dma((1,)), dma((KV_HEADS,)), dma((1,)), dma((1,))]
        + [dma((2,)), dma((2,)), dma((1,)), dma((1,)), dma((4,))],
        compiler_params=pltpu.CompilerParams(
            collective_id=0, has_side_effects=True, vmem_limit_bytes=60 * 1024 * 1024
        ),
        name="snap",
    )(cached_keys, cached_values, wq, kept_count, kept_entry.reshape(1, slots), row_owner.reshape(1, slots))
    return (
        importance,
        rows[:, :cap].reshape(n * cap, 2 * HEAD_DIM),
        score[:, 0, :cap].reshape(n * cap).astype(bf16),
    )


def solution(mesh):
    n = mesh.shape["seq"]
    split = P(("rep", "seq"))
    wide = P(("rep", "seq"), None)
    return jax.shard_map(
        functools.partial(per_device, n),
        mesh=mesh,
        in_specs=(wide, wide, wide, split, split, split),
        out_specs=(P("rep", "seq"), wide, split),
        check_vma=False,
    )
```

```python
import functools

import jax
import jax.numpy as jnp
from jax import lax
from jax.experimental import pallas as pl
from jax.experimental.pallas import tpu as pltpu
from jax.sharding import PartitionSpec as P

KV_HEADS = 8
GROUP = 8
HEAD_DIM = 128
POOL = 7
LOG2E = 1.4426950408889634
LANES = 128
MESH = pl.DeviceIdType.MESH
NT = (((1,), (1,)), ((), ()))


def iota(shape, dim):
    return lax.broadcasted_iota(jnp.int32, shape, dim)


def kernel(
    n, cap, cap_pad, pool_scale,
    keys_hbm, vals_hbm, wq_hbm, count_ref, entry_ref, owner_ref,
    imp_ref, rows_out, score_out,
    keys, vals, qall, ebuf, stat, stat_in, stat_all, glob, rows_send, onehot, head_hot, mass, halo, ssend, srecv,
    zs, zr, ys, yr, bs, br, ts, tr, gs, gr, rs, rr, hs, hr, ss, sr, ls, es, er,
):
    G = KV_HEADS
    me = lax.axis_index("seq")
    A = n // 4
    a, b, c = me // 4, (me // 2) % 2, me % 2
    slots = entry_ref.shape[0]
    positions = keys.shape[0]
    out_slots = n * cap_pad
    qrows = qall.shape[4]
    scale = HEAD_DIM ** (-0.5)
    per_owner = n // G

    def stat_owner(g):
        return (g * per_owner + n // 2) % n

    def to(index):
        return {"seq": index}

    def remote(src, dst, ssem, rsem, index):
        return pltpu.make_async_remote_copy(
            src_ref=src, dst_ref=dst, send_sem=ssem, recv_sem=rsem,
            device_id=to(index), device_id_type=MESH,
        )

    def drain(region, sem):
        pltpu.make_async_copy(region, region, sem).wait()

    key_copy = pltpu.make_async_copy(keys_hbm, keys, ls.at[0])
    val_copy = pltpu.make_async_copy(vals_hbm, vals, ls.at[1])
    own_q = pltpu.make_async_copy(wq_hbm, qall.at[:, c, b, a], ls.at[2])
    own_q.start()
    key_copy.start()
    val_copy.start()
    barrier = pltpu.get_barrier_semaphore()

    @pl.loop(1, n)
    def _(k):
        pl.semaphore_signal(barrier, inc=1, device_id=to(lax.rem(me + k, n)), device_id_type=MESH)

    entry = entry_ref[...].reshape(1, slots)
    owner = owner_ref[...].reshape(1, slots)
    live = iota((1, slots), 1) < count_ref[0]
    owner_live = jnp.where(live, owner, -1)
    member = jnp.where(iota((n, slots), 0) == owner_live, 1.0, 0.0)
    before = jnp.where(iota((slots, slots), 0) < iota((slots, slots), 1), 1.0, 0.0).astype(jnp.bfloat16)
    earlier = jnp.dot(member.astype(jnp.bfloat16), before, preferred_element_type=jnp.float32)
    rank = jnp.sum(member * earlier, axis=0, keepdims=True)
    target = jnp.where(live, owner * cap_pad + rank.astype(jnp.int32), -1)
    head = jnp.zeros((1, slots), jnp.int32)
    for h in range(1, G):
        head = head + jnp.where(entry >= h * positions, 1, 0)
    token = entry - head * positions
    token_f = (token + 1).astype(jnp.float32)
    head_f = head.astype(jnp.float32)
    head_sel = jnp.where(iota((G, slots), 0) == head, 1.0, 0.0).astype(jnp.bfloat16)
    blk = 256
    for i in range(out_slots // blk):
        hit = (iota((blk, slots), 0) + i * blk) == target
        tok = jnp.sum(jnp.where(hit, token_f, 0.0), axis=1, keepdims=True).astype(jnp.int32) - 1
        onehot[i * blk:(i + 1) * blk, :] = jnp.where(
            iota((blk, positions), 1) == tok, 1.0, 0.0
        ).astype(jnp.bfloat16)
        hit_b = jnp.where(hit, 1.0, 0.0).astype(jnp.bfloat16)
        head_hot[:, i * blk:(i + 1) * blk] = lax.dot_general(
            head_sel, hit_b, NT, preferred_element_type=jnp.float32
        )

    own_q.wait()
    pl.semaphore_wait(barrier, n - 1)

    @pl.loop(0, G)
    def _(g):
        @pl.loop(1, A)
        def _(k):
            peer = lax.rem(a + k, A) * 4 + b * 2 + c
            remote(qall.at[g, c, b, a], qall.at[g, c, b, a], zs.at[g], zr.at[g], peer).start()

    key_copy.wait()
    val_copy.wait()

    for i in range(out_slots // blk):
        hit = (iota((blk, slots), 0) + i * blk) == target
        hcol = jnp.sum(jnp.where(hit, head_f, 0.0), axis=1, keepdims=True).astype(jnp.int32)
        hcol = jnp.broadcast_to(hcol, (blk, HEAD_DIM))
        pick = onehot[i * blk:(i + 1) * blk, :]
        for side, source in enumerate((keys, vals)):
            got = jnp.dot(pick, source[...], preferred_element_type=jnp.float32)
            chosen = jnp.zeros((blk, HEAD_DIM), jnp.float32)
            for h in range(G):
                chosen = jnp.where(hcol == h, got[:, h * HEAD_DIM:(h + 1) * HEAD_DIM], chosen)
            rows_send[
                i * blk:(i + 1) * blk,
                side * HEAD_DIM:(side + 1) * HEAD_DIM,
            ] = chosen.astype(jnp.bfloat16)

    def join(g, gathered):
        gathered[me] = stat[g]
        top = gathered[0, 0]
        for d in range(1, n):
            top = jnp.maximum(top, gathered[d, 0])
        total = jnp.zeros_like(top)
        for d in range(n):
            total = total + gathered[d, 1] * jnp.exp(gathered[d, 0] - top)
        glob[g, 0] = top
        glob[g, 1] = 1.0 / total

    def combine(g):
        @pl.when(me == stat_owner(g))
        def _():
            drain(stat_in.at[pl.ds(0, n - 1)], tr.at[0])
            join(g, stat_in)

            @pl.loop(1, n)
            def _(k):
                remote(glob.at[g], glob.at[g], gs.at[0], gr.at[g], lax.rem(me + k, n)).start()

    chunk = 2 * LANES
    tblk = 256

    def compute(g):
        group_q = qall.at[g].reshape(qall.shape[1] * qall.shape[2] * A * qrows, HEAD_DIM)
        total_rows = group_q.shape[0]
        key_cols = pl.ds(pl.multiple_of(g * HEAD_DIM, HEAD_DIM), HEAD_DIM)

        @pl.loop(0, total_rows // chunk)
        def _(j):
            qs = group_q[pl.ds(pl.multiple_of(j * chunk, chunk), chunk), :]
            lanes = pl.ds(pl.multiple_of(j * chunk, chunk), chunk)
            top8 = None
            for t in range(positions // tblk):
                s = lax.dot_general(
                    keys[t * tblk:(t + 1) * tblk, key_cols], qs, NT, preferred_element_type=jnp.float32
                )
                ebuf[g, t * tblk:(t + 1) * tblk, lanes] = s
                part = jnp.max(s.reshape(tblk // 8, 8, chunk), axis=0)
                top8 = part if top8 is None else jnp.maximum(top8, part)
            top = jnp.max(top8, axis=0, keepdims=True)
            sum8 = jnp.zeros((8, chunk), jnp.float32)
            for t in range(positions // tblk):
                s = ebuf[g, t * tblk:(t + 1) * tblk, lanes]
                e = jnp.exp2((s - top) * (scale * LOG2E))
                ebuf[g, t * tblk:(t + 1) * tblk, lanes] = e
                sum8 = sum8 + jnp.sum(e.reshape(tblk // 8, 8, chunk), axis=0)
            total = jnp.sum(sum8, axis=0, keepdims=True)
            top = top * scale
            for i in range(chunk // LANES):
                stat[g, 0, pl.ds(j * (chunk // LANES) + i, 1), :] = top[:, i * LANES:(i + 1) * LANES]
                stat[g, 1, pl.ds(j * (chunk // LANES) + i, 1), :] = total[:, i * LANES:(i + 1) * LANES]

        dest = stat_owner(g)

        @pl.when((g < G - 1) & (me != dest))
        def _():
            remote(stat.at[g], stat_in.at[me], ts.at[g], tr.at[0], dest).start()

        @pl.when(g == G - 1)
        def _():
            @pl.loop(1, n)
            def _(k):
                remote(stat.at[g], stat_all.at[me], es.at[0], er.at[0], lax.rem(me + k, n)).start()

    rows3 = rows_send.reshape(n, cap_pad, 2 * HEAD_DIM)
    own_rows = pltpu.make_async_copy(rows3.at[me], rows_out.at[me], ls.at[3])
    own_rows.start()
    mid_peer = a * 4 + (1 - b) * 2 + c
    core_peer = a * 4 + b * 2 + (1 - c)

    lag = 5

    @pl.loop(0, G + 2)
    def _(step):
        @pl.when(step < G)
        def _():
            g = step
            drain(qall.at[g, c, b, pl.ds(0, A - 1)], zr.at[g])
            remote(qall.at[g, c, b], qall.at[g, c, b], ys.at[g], yr.at[g], mid_peer).start()

        @pl.when(step == G // 2)
        def _():
            @pl.loop(1, n)
            def _(k):
                peer = lax.rem(me + k, n)
                remote(rows3.at[peer], rows_out.at[me], rs.at[0], rr.at[0], peer).start()

        @pl.when((step >= 1) & (step < G + 1))
        def _():
            g = step - 1
            drain(qall.at[g, c, 1 - b], yr.at[g])
            remote(qall.at[g, c], qall.at[g, c], bs.at[g], br.at[g], core_peer).start()

        @pl.when((step >= 2) & (step < G + 2))
        def _():
            g = step - 2
            drain(qall.at[g, 1 - c], br.at[g])
            compute(g)

        @pl.when(step >= lag)
        def _():
            combine(step - lag)

    @pl.loop(G + 2 - lag, G - 1)
    def _(g):
        combine(g)

    ones = jnp.ones((8, LANES), jnp.float32)

    @pl.loop(0, G)
    def _(g):
        @pl.when((g < G - 1) & (me != stat_owner(g)))
        def _():
            drain(glob.at[g], gr.at[g])

        @pl.when(g == G - 1)
        def _():
            drain(stat_all.at[pl.ds(0, n - 1)], er.at[0])
            join(g, stat_all)

        weight = jnp.exp(stat[g, 0] - glob[g, 0]) * glob[g, 1]
        for t in range(positions // LANES):
            acc = ebuf[g, t * LANES:(t + 1) * LANES, 0:LANES] * weight[0:1, :]
            for k in range(1, weight.shape[0]):
                acc = acc + ebuf[g, t * LANES:(t + 1) * LANES, k * LANES:(k + 1) * LANES] * weight[k:k + 1, :]
            line = lax.dot_general(
                ones, acc, NT, preferred_element_type=jnp.float32, precision=lax.Precision.HIGHEST
            )
            mass[g, :, t * LANES:(t + 1) * LANES] = line[0:1, :]

    halo[0] = jnp.zeros((G, LANES), jnp.float32)
    halo[1] = jnp.zeros((G, LANES), jnp.float32)
    column = jnp.concatenate([mass[g] for g in range(G)], axis=0)
    halo[4] = column[:, 0:LANES]
    halo[5] = column[:, positions - LANES:]
    low_copy = remote(halo.at[4], halo.at[3], hs.at[0], hr.at[0], lax.rem(me + n - 1, n))
    high_copy = remote(halo.at[5], halo.at[2], hs.at[1], hr.at[1], lax.rem(me + 1, n))

    @pl.when(me > 0)
    def _():
        low_copy.start()

    @pl.when(me < n - 1)
    def _():
        high_copy.start()

    @pl.when(me > 0)
    def _():
        drain(halo.at[2], hr.at[1])
        halo[0] = halo[2]

    @pl.when(me < n - 1)
    def _():
        drain(halo.at[3], hr.at[0])
        halo[1] = halo[3]

    padded = jnp.concatenate([halo[0], column, halo[1]], axis=1)
    width = padded.shape[1]
    pooled = padded
    for o in range(1, POOL // 2 + 1):
        pooled = pooled + pltpu.roll(padded, o, 1) + pltpu.roll(padded, width - o, 1)
    importance = pooled[:, LANES:LANES + positions] * pool_scale
    imp_ref[...] = importance

    got = lax.dot_general(
        importance.astype(jnp.bfloat16), onehot[...], NT, preferred_element_type=jnp.float32
    )
    line = jnp.sum(got * head_hot[...], axis=0, keepdims=True)
    owner_of = iota((n, out_slots), 1) - iota((n, out_slots), 0) * cap_pad
    spread = jnp.where((owner_of >= 0) & (owner_of < cap_pad), line, 0.0).astype(jnp.bfloat16)
    row_id, lane_id = iota((out_slots, LANES), 0), iota((out_slots, LANES), 1)
    fold = (row_id - lane_id) % cap_pad == 0
    fold = jnp.where(fold & (lane_id < cap_pad), 1.0, 0.0).astype(jnp.bfloat16)
    table = jnp.dot(spread, fold, preferred_element_type=jnp.float32)
    for k in range(n):
        ssend[k] = table[k:k + 1, :]

    @pl.loop(1, n)
    def _(k):
        peer = lax.rem(me + k, n)
        remote(ssend.at[peer], srecv.at[me], ss.at[0], sr.at[0], peer).start()

    own_rows.wait()
    drain(rows_out.at[pl.ds(0, n - 1)], rr.at[0])
    drain(rows3.at[pl.ds(0, n - 1)], rs.at[0])

    @pl.loop(0, G)
    def _(g):
        drain(qall.at[g, c, b, pl.ds(0, A - 1)], zs.at[g])
        drain(qall.at[g, c, b], ys.at[g])
        drain(qall.at[g, c], bs.at[g])

        @pl.when((g < G - 1) & (me != stat_owner(g)))
        def _():
            drain(stat.at[g], ts.at[g])

        @pl.when((g < G - 1) & (me == stat_owner(g)))
        def _():
            drain(stat_in.at[pl.ds(0, n - 1)], gs.at[0])

    @pl.when(me > 0)
    def _():
        drain(halo.at[4], hs.at[0])

    @pl.when(me < n - 1)
    def _():
        drain(halo.at[5], hs.at[1])

    drain(stat_all.at[pl.ds(0, n - 1)], es.at[0])
    drain(ssend.at[pl.ds(0, n - 1)], ss.at[0])
    drain(srecv.at[pl.ds(0, n - 1)], sr.at[0])
    srecv[me] = ssend[me]
    score_out[...] = srecv[...]


def finish(cap, imp_in, rows_in, score_in, imp_ref, rows_ref, score_ref):
    n = rows_in.shape[0]
    imp_ref[...] = imp_in[...]
    rows_ref[...] = rows_in[:, 0:cap, :]
    table = jnp.concatenate([score_in[k] for k in range(n)], axis=0).astype(jnp.bfloat16)
    column = iota((LANES, n * cap), 1) - iota((LANES, n * cap), 0)
    unfold = jnp.where(column % cap == 0, 1.0, 0.0)
    unfold = jnp.where(iota((LANES, n * cap), 0) < cap, unfold, 0.0).astype(jnp.bfloat16)
    wide = jnp.dot(table, unfold, preferred_element_type=jnp.float32)
    within = iota((n, n * cap), 1) - iota((n, n * cap), 0) * cap
    line = jnp.sum(jnp.where((within >= 0) & (within < cap), wide, 0.0), axis=0, keepdims=True)
    score_ref[...] = line.astype(jnp.bfloat16).reshape(n * cap)


def per_device(n, cached_keys, cached_values, window_queries, kept_count, kept_entry, row_owner):
    positions, width = cached_keys.shape
    slots = kept_entry.shape[0]
    cap = slots // n
    cap_pad = -(-cap // 16) * 16
    query_rows = window_queries.shape[0]
    heads = window_queries.shape[1] // HEAD_DIM
    group = heads // KV_HEADS
    window = query_rows * n
    qrows = query_rows * group
    lane_rows = n * qrows // LANES
    wq = (
        window_queries.reshape(query_rows, heads, HEAD_DIM)
        .transpose(1, 0, 2)
        .reshape(KV_HEADS, qrows, HEAD_DIM)
    )
    pool_scale = n * positions / (group * window * POOL)
    any_spec = pl.BlockSpec(memory_space=pl.ANY)
    vmem = pl.BlockSpec(memory_space=pltpu.VMEM)
    dma = pltpu.SemaphoreType.DMA
    A = n // 4
    f32, bf16 = jnp.float32, jnp.bfloat16
    importance, rows, score = pl.pallas_call(
        functools.partial(kernel, n, cap, cap_pad, pool_scale),
        out_shape=(
            jax.ShapeDtypeStruct((KV_HEADS, positions), f32),
            jax.ShapeDtypeStruct((n, cap_pad, 2 * HEAD_DIM), bf16),
            jax.ShapeDtypeStruct((n, 1, LANES), f32),
        ),
        in_specs=[any_spec, any_spec, any_spec, pl.BlockSpec(memory_space=pltpu.SMEM), vmem, vmem],
        out_specs=(vmem, any_spec, vmem),
        scratch_shapes=[
            pltpu.VMEM((positions, width), bf16),
            pltpu.VMEM((positions, width), bf16),
            pltpu.VMEM((KV_HEADS, 2, 2, A, qrows, HEAD_DIM), bf16),
            pltpu.VMEM((KV_HEADS, positions, n * qrows), f32),
            pltpu.VMEM((KV_HEADS, 2, lane_rows, LANES), f32),
            pltpu.VMEM((n, 2, lane_rows, LANES), f32),
            pltpu.VMEM((n, 2, lane_rows, LANES), f32),
            pltpu.VMEM((KV_HEADS, 2, lane_rows, LANES), f32),
            pltpu.VMEM((n * cap_pad, 2 * HEAD_DIM), bf16),
            pltpu.VMEM((n * cap_pad, positions), bf16),
            pltpu.VMEM((KV_HEADS, n * cap_pad), f32),
            pltpu.VMEM((KV_HEADS, 1, positions), f32),
            pltpu.VMEM((6, KV_HEADS, LANES), f32),
            pltpu.VMEM((n, 1, LANES), f32),
            pltpu.VMEM((n, 1, LANES), f32),
        ]
        + [dma((KV_HEADS,))] * 6
        + [dma((KV_HEADS,)), dma((1,)), dma((1,)), dma((KV_HEADS,)), dma((1,)), dma((1,))]
        + [dma((2,)), dma((2,)), dma((1,)), dma((1,)), dma((4,)), dma((1,)), dma((1,))],
        compiler_params=pltpu.CompilerParams(
            collective_id=0, has_side_effects=True, vmem_limit_bytes=60 * 1024 * 1024
        ),
        name="snap",
    )(cached_keys, cached_values, wq, kept_count, kept_entry, row_owner)
    importance, rows, score = pl.pallas_call(
        functools.partial(finish, cap),
        out_shape=(
            jax.ShapeDtypeStruct((KV_HEADS, positions), f32),
            jax.ShapeDtypeStruct((n, cap, 2 * HEAD_DIM), bf16),
            jax.ShapeDtypeStruct((n * cap,), bf16),
        ),
        in_specs=[vmem, vmem, vmem],
        out_specs=(vmem, vmem, vmem),
        name="finish",
    )(importance, rows, score)
    return importance, rows.reshape(n * cap, 2 * HEAD_DIM), score


def solution(mesh):
    n = mesh.shape["seq"]
    split = P(("rep", "seq"))
    wide = P(("rep", "seq"), None)
    return jax.shard_map(
        functools.partial(per_device, n),
        mesh=mesh,
        in_specs=(wide, wide, wide, split, split, split),
        out_specs=(P("rep", "seq"), wide, split),
        check_vma=False,
    )
```
